512 devices in a mesh: dp: 64 (over x, y, core), tensor: 8 (over z).
Axes of the slice: x: 4, y: 8, z: 8, core: 2. Of those that a mesh axis runs over, the one named last changes fastest.
Arguments:
- features: bfloat16 [65536, 4096], P(('dp', 'tensor')), may hold values from -20 to 20
- key_grads: bfloat16 [65536, 1024], P('dp', 'tensor'), may hold values from -20 to 20
- error_in: bfloat16 [64, 4096, 1024], P('dp', None, 'tensor'), may hold values from -24 to 24
- selected: int32 [64, 8, 128], P('dp', 'tensor'), may hold values from 0 to 4095, as said below
- bin_edges: int32 [17], replicated, may hold values from 0 to 4096, as said below
- threshold: int32 [1], replicated, may hold values from 1 to 15
- moment: float32 [4096, 1024], P('dp', 'tensor'), may hold values from -2 to 2
- second: float32 [4096, 1024], P('dp', 'tensor'), may hold values from 0.05 to 2
- master: float32 [4096, 1024], P('dp', 'tensor'), may hold values from -0.0625 to 0.0625
Outputs:
- keys: bfloat16 [65536, 1024], P('dp', 'tensor')
- error_out: bfloat16 [64, 4096, 1024], P('dp', None, 'tensor')
- moment_new: float32 [4096, 1024], P('dp', 'tensor')
- second_new: float32 [4096, 1024], P('dp', 'tensor')
- master_new: float32 [4096, 1024], P('dp', 'tensor')
The draws below stay inside these ranges and needn't reach their ends.
Inputs may be any that keep to these rules, and one draw needn't show every extreme that they name: Each device's 128 rows are distinct; the rows o * 64 to (o + 1) * 64 - 1 form owner o's region, and one device's row of selected names at most 6 rows of one region; there is one region, the same for every row of selected, that receives exactly 6 blocks from each row; every other region receives at most 6 from a row. bin_edges[0] = 0, bin_edges[16] = 4096, strictly increasing.
All inputs are finite; a program needn't handle non-finite values.
Results may differ from the reference program's by a relative error of at most 0.001.
The reference program's roundings to bfloat16 on the way (of `weight`) count: a program that leaves them out, or rounds other values in their place, can miss the bound.
Values may be sent and summed in bfloat16 or wider, within the bound.
A program may use at most 64 MiB of HBM per device.

```python
import math
import jax
import jax.numpy as jnp
from jax import lax

ROWS = 4096
HD = 128
TOK_DEV = 1024
CAP = 6
BINS = 16
COLS = 1024
TOKENS = 65536
KEEP = 128
REGION = 64
N_DP = 64
N_TENSOR = 8


def draw_features(key, part):
    freq = jax.random.randint(jax.random.fold_in(key, 21), (), 1, 4).astype(jnp.float32)
    phase = jax.random.uniform(jax.random.fold_in(key, 22), (), jnp.float32, 0.0, 6.283)
    place = jnp.arange(ROWS, dtype=jnp.float32) / ROWS
    depth = 0.45
    base = jnp.clip(jax.random.normal(jax.random.fold_in(key, 23), (TOKENS, ROWS), jnp.float32), -6.0, 6.0)
    profile = jnp.exp(2.302585 * depth * jnp.sin(6.283185 * freq * place + phase))
    return (base * profile[None, :]).astype(jnp.bfloat16)


def draw_key_grads(key, part):
    rise = 1.0 + 2.0 * jnp.arange(TOKENS, dtype=jnp.float32) / (TOKENS - 1)
    level = 4.0 / TOK_DEV ** 0.5
    values = jax.random.normal(jax.random.fold_in(key, 11), (TOKENS, COLS), jnp.float32)
    return jnp.clip(values * rise[:, None] * level, -19.5, 19.5).astype(jnp.bfloat16)


def pick_blocks(device_key, hot_owner):
    bias_key, noise_key, perm_key, order_key = jax.random.split(device_key, 4)
    bias = jax.random.randint(bias_key, (N_DP, 1), 0, 4).astype(jnp.int32) * 4096
    noise = jax.random.randint(noise_key, (N_DP, CAP), 0, 4096).astype(jnp.int32)
    owner_column = jnp.arange(N_DP, dtype=jnp.int32)[:, None]
    score = jnp.where(owner_column == hot_owner, -1, bias + noise)
    flat = score.reshape(-1) * (N_DP * CAP) + jnp.arange(N_DP * CAP, dtype=jnp.int32)
    top_values, picked = lax.top_k(flat, KEEP - CAP)
    picked = picked.astype(jnp.int32)
    owners = jnp.concatenate([picked // CAP, jnp.full((CAP,), hot_owner, jnp.int32)])
    slots = jnp.concatenate([picked % CAP, jnp.arange(CAP, dtype=jnp.int32)])
    perms = jax.vmap(lambda k: jax.random.permutation(k, REGION).astype(jnp.int32))(jax.random.split(perm_key, N_DP))
    blocks = owners * REGION + perms[owners, slots]
    return jax.random.permutation(order_key, blocks).astype(jnp.int32)


def draw_selected(key, part):
    hot_owner = jax.random.randint(jax.random.fold_in(key, 1), (), 0, N_DP).astype(jnp.int32)
    device_keys = jax.random.split(jax.random.fold_in(key, 2), N_DP * N_TENSOR)
    picks = jax.vmap(pick_blocks, in_axes=(0, None))(device_keys, hot_owner)
    return picks.reshape(N_DP, N_TENSOR, KEEP).astype(jnp.int32)


def draw_bin_edges(key, part):
    order = jax.random.permutation(jax.random.fold_in(key, 5), ROWS - 1).astype(jnp.int32)
    inner = jnp.sort(order[:BINS - 1] + 1)
    return jnp.concatenate([jnp.zeros((1,), jnp.int32), inner, jnp.full((1,), ROWS, jnp.int32)])


def block_levels(key, shape, cuts, least, high):
    level = 1.0
    for axis_at, shards_of in cuts:
        draws = jax.random.uniform(jax.random.fold_in(jax.random.fold_in(key, 6), axis_at), (shards_of,), jnp.float32, least / len(cuts), high / len(cuts))
        level = level * jnp.repeat(jnp.exp(draws), shape[axis_at] // shards_of).reshape((-1,) + (1,) * (len(shape) - 1 - axis_at))
    return level


def gaussian(stream_key, shape, spread, most, cuts=(), held_as=jnp.bfloat16):
    array = jax.random.normal(stream_key, shape, jnp.float32) * spread
    if len(cuts) > 0:
        array = block_levels(stream_key, shape, cuts, -0.22, 0.18) * array
    return jnp.clip(array, min=-most, max=most).astype(held_as)


def setup_inputs(seed: int = 0) -> dict:
    seeds = jax.random.split(jax.random.key(seed), 10)
    return {
        "features": draw_features(jax.random.fold_in(seeds[9], 71), 0),
        "key_grads": draw_key_grads(jax.random.fold_in(seeds[9], 71), 0),
        "error_in": gaussian(seeds[2], (N_DP, ROWS, COLS), 4.0, 24.0, ((0, 64), (2, 8))),
        "selected": draw_selected(jax.random.fold_in(seeds[9], 71), 0),
        "bin_edges": draw_bin_edges(jax.random.fold_in(seeds[9], 71), 0),
        "threshold": jax.random.randint(seeds[5], (1,), 1, BINS).astype(jnp.int32),
        "moment": gaussian(seeds[6], (ROWS, COLS), 0.3, 2.0, ((0, 64), (1, 8)), jnp.float32),
        "second": jnp.clip(jnp.exp(math.log(2.0) - 3.6888794 * jax.random.uniform(seeds[7], (ROWS, COLS), jnp.float32) ** block_levels(seeds[7], (ROWS, COLS), ((0, 64), (1, 8)), -0.2, 0.2)), 0.05, 2.0),
        "master": gaussian(seeds[8], (ROWS, COLS), (2 * ROWS) ** -0.5, 0.0625, ((0, 64), (1, 8)), jnp.float32),
    }


beta_first = 0.9
beta_second = 0.95
learn_rate = 0.001
decay_rate = 0.1
epsilon = 1e-06
adam_epsilon = 1e-08
step_count = 10.0

def reference(features, key_grads, error_in, selected, bin_edges, threshold, moment, second, master):
    highest = lax.Precision.HIGHEST
    feats = features.reshape(N_DP, TOK_DEV, ROWS)
    grads_in = key_grads.reshape(N_DP, TOK_DEV, COLS)

    def local_sum(triple):
        return jnp.dot(triple[0].T, triple[1], preferred_element_type=jnp.float32) + triple[2].astype(jnp.float32)
    summed = lax.map(local_sum, (feats, grads_in, error_in))
    blocks = summed.reshape(N_DP, ROWS, N_TENSOR, HD)
    squares = lax.optimization_barrier(jnp.sum(blocks * blocks, axis=3))
    row_ids = jnp.arange(ROWS, dtype=jnp.int32)
    member = ((row_ids[:, None] >= bin_edges[None, :BINS]) & (row_ids[:, None] < bin_edges[None, 1:])).astype(jnp.float32)
    energy = jnp.dot(member.T, lax.optimization_barrier(jnp.sum(squares, axis=0)), precision=highest)
    widths = (bin_edges[1:] - bin_edges[:BINS]).astype(jnp.float32)
    levels = jnp.arange(BINS, dtype=jnp.int32)
    normal = 1.0 / jnp.sqrt(energy / (N_DP * HD * widths[:, None]) + epsilon)
    scale = jnp.where((levels >= threshold[0])[:, None], normal, jnp.ones_like(normal))
    row_scale = jnp.dot(member, scale, precision=highest)
    device_index = jnp.arange(N_DP, dtype=jnp.int32)[:, None, None]
    head_index = jnp.arange(N_TENSOR, dtype=jnp.int32)[None, :, None]
    chosen = jnp.zeros((N_DP, N_TENSOR, ROWS), jnp.float32).at[device_index, head_index, selected].set(1.0)
    chosen = jnp.transpose(chosen, (0, 2, 1))
    kept = blocks * chosen[..., None]
    error_out = (blocks - kept).reshape(N_DP, ROWS, COLS).astype(jnp.bfloat16)
    grad = lax.optimization_barrier(jnp.sum(kept * row_scale[None, :, :, None], axis=0)).reshape(ROWS, COLS)
    moment_new = beta_first * moment + (1.0 - beta_first) * grad
    second_new = beta_second * second + (1.0 - beta_second) * grad * grad
    first_hat = moment_new / (1.0 - beta_first ** step_count)
    second_hat = second_new / (1.0 - beta_second ** step_count)
    master_new = master - learn_rate * (first_hat / (jnp.sqrt(second_hat) + adam_epsilon) + decay_rate * master)
    weight = master_new.astype(jnp.bfloat16)

    def project(rows_block):
        return jnp.dot(rows_block, weight, preferred_element_type=jnp.float32)
    keys = lax.map(project, feats).reshape(TOKENS, COLS).astype(jnp.bfloat16)
    return (keys, error_out, moment_new, second_new, master_new)
```

```python
import jax
import jax.numpy as jnp
from jax import lax
from jax.experimental import pallas as pl
from jax.experimental.pallas import tpu as pltpu
from jax.sharding import PartitionSpec as P

MESH = pl.DeviceIdType.MESH
F32 = jnp.float32
BF16 = jnp.bfloat16

ROWS = 4096
HD = 128
NZ = 8
NDP = 64
NX, NY = 4, 8
REGION = 64
TOK = 128
NCH = 8
CW = ROWS // NCH
NBINS = 16

beta_first = 0.9
beta_second = 0.95
learn_rate = 0.001
decay_rate = 0.1
epsilon = 1e-06
adam_epsilon = 1e-08
step_count = 10.0

NEAR_FIRST = (0, 1, 7, 2, 6, 3, 5, 4)


def dot(a, b):
    return lax.dot_general(a, b, (((1,), (0,)), ((), ())), preferred_element_type=F32)


def dot_t(a, b):
    return lax.dot_general(a, b, (((0,), (0,)), ((), ())), preferred_element_type=F32)


def split3(v):
    high = v.astype(BF16)
    rest = v - high.astype(F32)
    mid = rest.astype(BF16)
    low = (rest - mid.astype(F32)).astype(BF16)
    return high, mid, low


def kernel(
    feat, kg, err_in, sel_ref, edges, thr, mom, sec, mas,
    keys_out, err_out, mom_out, sec_out, mas_out,
    fbuf, gbuf, ein, acc, maskb, memb, vbuf, errb, ebins, tiles, got, eng, wbuf, kacc, kout, state, news,
    lsem, isem, osem, zsend, zrecv, tsend, trecv, gsend, grecv, wsend, wa, wb, wc,
):
    z = lax.axis_index("tensor")
    me = lax.axis_index("dp")
    right, left = lax.rem(z + 1, NZ), lax.rem(z + NZ - 1, NZ)

    def load(c):
        return pltpu.make_async_copy(
            feat.at[:, pl.ds(pl.multiple_of(c * CW, CW), CW)], fbuf.at[z, c], lsem.at[c]
        )

    for c in range(NCH):
        load(c).start()
    loads = [
        pltpu.make_async_copy(kg, gbuf, isem.at[0]),
        pltpu.make_async_copy(err_in.at[0], ein, isem.at[1]),
        pltpu.make_async_copy(mom, state.at[0], isem.at[2]),
        pltpu.make_async_copy(sec, state.at[1], isem.at[3]),
        pltpu.make_async_copy(mas, state.at[2], isem.at[4]),
    ]
    for copy in loads:
        copy.start()

    barrier = pltpu.get_barrier_semaphore()
    for near in (left, right):
        pl.semaphore_signal(barrier, inc=1, device_id={"tensor": near}, device_id_type=MESH)

    def greet(k, carry):
        pl.semaphore_signal(
            barrier, inc=1, device_id={"dp": lax.rem(me + k, NDP)}, device_id_type=MESH
        )
        return carry

    lax.fori_loop(1, NDP, greet, 0)
    pl.semaphore_wait(barrier, NDP + 1)

    def hop(way, h, c, origin):
        return pltpu.make_async_remote_copy(
            src_ref=fbuf.at[origin, c],
            dst_ref=fbuf.at[origin, c],
            send_sem=zsend.at[way, 0 if h < 4 else 1],
            recv_sem=zrecv.at[way, h - 1, c],
            device_id={"tensor": right if way == 0 else left},
            device_id_type=MESH,
        )

    def first(c, carry):
        load(c).wait()
        hop(0, 1, c, z).start()
        hop(1, 1, c, z).start()
        return carry

    lax.fori_loop(0, NCH, first, 0)

    sel = sel_ref[0]
    sub = lax.broadcasted_iota(jnp.int32, (HD, HD), 0)
    lane = lax.broadcasted_iota(jnp.int32, (HD, HD), 1)
    group_hot = jnp.where(sub[:32] == lax.shift_right_logical(sel, 7), 1.0, 0.0).astype(BF16)
    place_hot = jnp.where(sub == lax.bitwise_and(sel, 127), 1.0, 0.0).astype(BF16)
    chosen = lax.dot_general(
        group_hot, place_hot, (((1,), (1,)), ((), ())), preferred_element_type=F32
    )
    same = lax.shift_right_logical(sub, 6) == lax.shift_right_logical(lane, 6)
    before = jnp.where(same & (sub < lane), 1.0, 0.0).astype(BF16)
    rank = dot(chosen.astype(BF16), before)
    half = lax.shift_right_logical(lane[:32], 6).astype(F32) * 8.0
    slots = jnp.where(chosen > 0.5, half + rank, -1.0)
    for g in range(32):
        vbuf[g] = slots[g : g + 1]

    bin_of = lax.broadcasted_iota(jnp.int32, (NBINS, CW), 0)
    low_edge = jnp.zeros((NBINS, CW), jnp.int32)
    high_edge = jnp.zeros((NBINS, CW), jnp.int32)
    for b in range(NBINS):
        low_edge = jnp.where(bin_of == b, edges[b], low_edge)
        high_edge = jnp.where(bin_of == b, edges[b + 1], high_edge)
    row_of = lax.broadcasted_iota(jnp.int32, (NBINS, CW), 1)
    ones = jnp.ones((HD, HD), BF16)
    row_col = lax.broadcasted_iota(jnp.int32, (CW, HD), 0)

    for copy in loads[:2]:
        copy.wait()

    def shard_of(origin):
        return gbuf[pl.ds(pl.multiple_of(origin * TOK, TOK), TOK), :]

    def prepare(c, carry):
        rows = row_of + c * CW
        memb[c] = jnp.where((rows >= low_edge) & (rows < high_edge), 1.0, 0.0).astype(BF16)
        hit = jnp.where(row_col + c * CW == sel, 1.0, 0.0).astype(BF16)
        maskb[c] = dot(hit, ones)
        acc[c] = ein[pl.ds(pl.multiple_of(c * CW, CW), CW), :].astype(F32) + dot_t(
            fbuf[z, c], shard_of(z)
        )
        return carry

    lax.fori_loop(0, NCH, prepare, 0)
    ebins[...] = jnp.zeros_like(ebins)

    for h in (1, 2, 3):
        low = lax.rem(z + NZ - h, NZ)
        high = lax.rem(z + h, NZ)

        def step(c, carry, h=h, low=low, high=high):
            hop(0, h, c, low).wait_recv()
            if h < 3:
                hop(0, h + 1, c, low).start()
            else:

                @pl.when(c < NCH // 2)
                def _():
                    hop(0, 4, c, low).start()

            hop(1, h, c, high).wait_recv()
            if h < 3:
                hop(1, h + 1, c, high).start()
            else:

                @pl.when(c >= NCH // 2)
                def _():
                    hop(1, 4, c, high).start()

            acc[c] = acc[c] + (
                dot_t(fbuf[low, c], shard_of(low)) + dot_t(fbuf[high, c], shard_of(high))
            )
            return carry

        lax.fori_loop(0, NCH, step, 0)

    far = lax.rem(z + NZ // 2, NZ)
    sub16 = lax.broadcasted_iota(jnp.int32, (16, HD), 0)
    slot16 = sub16.astype(F32)
    map_line = lax.rem(sub16, 8) == 6

    def block_copy(owner):
        return pltpu.make_async_remote_copy(
            src_ref=tiles.at[owner],
            dst_ref=got.at[me],
            send_sem=tsend,
            recv_sem=trecv,
            device_id={"dp": owner},
            device_id_type=MESH,
        )

    def err_copy(c):
        return pltpu.make_async_copy(
            errb.at[c], err_out.at[0, pl.ds(pl.multiple_of(c * CW, CW), CW), :], osem.at[c]
        )

    def finish(c):
        total = acc[c] + dot_t(fbuf[far, c], shard_of(far))
        errb[c] = jnp.where(maskb[c] > 0.5, 0.0, total).astype(BF16)
        err_copy(c).start()
        square = total * total
        top = square.astype(BF16)
        rest = (square - top.astype(F32)).astype(BF16)
        ebins[...] += dot(memb[c], top) + dot(memb[c], rest)
        parts = split3(total)
        for g in range(4):
            line = vbuf[c * 4 + g]
            pick = jnp.where(slot16 == line, 1.0, 0.0).astype(BF16)
            picked = [dot(pick, part[g * HD : (g + 1) * HD]) for part in parts]
            tile = jnp.where(map_line, line, (picked[0] + picked[1]) + picked[2])
            tiles[pl.ds(c * 8 + 2 * g, 2)] = tile.reshape(2, 8, HD)
        for j in range(8):
            owner = c * 8 + j

            @pl.when(owner != me)
            def _():
                block_copy(owner).start()

            @pl.when(owner == me)
            def _():
                got[me] = tiles[owner]

    def last(i, carry):
        for way in (0, 1):
            c = i + way * (NCH // 2)
            hop(way, 4, c, far).wait_recv()
            finish(c)
        return carry

    lax.fori_loop(0, NCH // 2, last, 0)

    lane16 = lax.broadcasted_iota(jnp.int32, (NBINS, HD), 1)
    bin_sum = jnp.sum(ebins[...], axis=1, keepdims=True)
    eng[me] = jnp.sum(jnp.where(lane16 == sub16, bin_sum, 0.0), axis=0, keepdims=True)

    def energy_copy(k):
        return pltpu.make_async_remote_copy(
            src_ref=eng.at[me],
            dst_ref=eng.at[me],
            send_sem=gsend,
            recv_sem=grecv,
            device_id={"dp": lax.rem(me + k, NDP)},
            device_id_type=MESH,
        )

    def tell(k, carry):
        energy_copy(k).start()
        return carry

    lax.fori_loop(1, NDP, tell, 0)

    for copy in loads[2:]:
        copy.wait()
    others = NDP - 1
    pltpu.make_async_copy(got.at[pl.ds(0, others)], got.at[pl.ds(0, others)], trecv).wait()
    parity = lax.rem(me, 2)
    block = got[...]
    want = (lax.broadcasted_iota(jnp.int32, (NDP, 8, HD), 1) + 8 * parity).astype(F32)
    hot = jnp.where(want == block[:, 6:7, :], 1.0, 0.0).astype(BF16).reshape(NDP * 8, HD)
    parts = split3(block.reshape(NDP * 8, HD))
    both = (dot_t(hot, parts[0]) + dot_t(hot, parts[1])) + dot_t(hot, parts[2])
    kept_sum = both[:REGION] + both[REGION:]

    lane1 = lax.broadcasted_iota(jnp.int32, (1, HD), 1)
    low1 = jnp.zeros((1, HD), jnp.int32)
    high1 = jnp.zeros((1, HD), jnp.int32)
    for b in range(NBINS):
        low1 = jnp.where(lane1 == b, edges[b], low1)
        high1 = jnp.where(lane1 == b, edges[b + 1], high1)
    width = jnp.where(lane1 < NBINS, high1 - low1, 1).astype(F32)
    own_row = me * REGION + lax.broadcasted_iota(jnp.int32, (REGION, HD), 0)
    in_bin = (own_row >= low1) & (own_row < high1)

    pltpu.make_async_copy(eng.at[pl.ds(0, others)], eng.at[pl.ds(0, others)], grecv).wait()
    energy = jnp.sum(eng[...], axis=0)
    normal = 1.0 / jnp.sqrt(energy / (float(NDP * HD) * width) + epsilon)
    scale = jnp.where(lane1 >= thr[0], normal, 1.0)
    row_scale = jnp.sum(jnp.where(in_bin, scale, 0.0), axis=1, keepdims=True)
    grad = kept_sum * row_scale
    moment_new = beta_first * state[0] + (1.0 - beta_first) * grad
    second_new = beta_second * state[1] + (1.0 - beta_second) * grad * grad
    first_hat = moment_new / (1.0 - beta_first**step_count)
    second_hat = second_new / (1.0 - beta_second**step_count)
    master = state[2]
    master_new = master - learn_rate * (
        first_hat / (jnp.sqrt(second_hat) + adam_epsilon) + decay_rate * master
    )
    wbuf[me] = master_new.astype(BF16)
    news[0] = moment_new
    news[1] = second_new
    news[2] = master_new

    x, y, core = me // (2 * NY), lax.rem(me // 2, NY), lax.rem(me, 2)
    partner = me + 1 - 2 * core

    def device(dx, dy, c):
        return (lax.rem(x + dx, NX) * NY + lax.rem(y + dy, NY)) * 2 + c

    def weight_copy(slot, to, sem):
        return pltpu.make_async_remote_copy(
            src_ref=wbuf.at[slot],
            dst_ref=wbuf.at[slot],
            send_sem=wsend,
            recv_sem=sem,
            device_id={"dp": to},
            device_id_type=MESH,
        )

    for k in NEAR_FIRST[1:]:
        weight_copy(me, device(0, k, core), wa.at[k]).start()
    outs = [
        pltpu.make_async_copy(news.at[0], mom_out, isem.at[5]),
        pltpu.make_async_copy(news.at[1], sec_out, isem.at[6]),
        pltpu.make_async_copy(news.at[2], mas_out, isem.at[7]),
    ]
    for k in NEAR_FIRST:
        slot = device(0, NY - k, core)
        if k:
            weight_copy(slot, partner, wa.at[k]).wait_recv()
        for d in (1, 3, 2):
            weight_copy(slot, device(d, 0, core), wb.at[d - 1, k]).start()
        weight_copy(slot, partner, wc.at[0, k]).start()
    for copy in outs:
        copy.start()

    kacc[...] = jnp.zeros_like(kacc)

    def project(d):
        for k in NEAR_FIRST:
            weight_copy(device(NX - d, NY - k, 1 - core), partner, wc.at[d, k]).wait_recv()
        where_x = lax.rem(x + NX - d, NX)
        for part in range(2):
            c = where_x * 2 + part
            weight = wbuf[pl.ds(c * 8, 8)].reshape(CW, HD)
            kacc[...] += dot(fbuf[:, c].reshape(NZ * TOK, CW), weight)

    done = 0
    for d in (1, 3, 2):
        for k in NEAR_FIRST:
            slot = device(NX - d, NY - k, core)
            weight_copy(slot, partner, wb.at[d - 1, k]).wait_recv()
            weight_copy(slot, partner, wc.at[d, k]).start()
        project(done)
        done = d
    project(done)
    kout[...] = kacc[...].astype(BF16)
    keys_copy = pltpu.make_async_copy(kout, keys_out, isem.at[0])
    keys_copy.start()

    for way in (0, 1):
        pltpu.make_async_copy(
            fbuf.at[pl.ds(0, 3)], fbuf.at[pl.ds(0, 3)], zsend.at[way, 0]
        ).wait()
        pltpu.make_async_copy(
            fbuf.at[0, pl.ds(0, 4)], fbuf.at[0, pl.ds(0, 4)], zsend.at[way, 1]
        ).wait()
    pltpu.make_async_copy(got.at[pl.ds(0, others)], got.at[pl.ds(0, others)], tsend).wait()
    pltpu.make_async_copy(eng.at[pl.ds(0, others)], eng.at[pl.ds(0, others)], gsend).wait()
    pltpu.make_async_copy(wbuf.at[pl.ds(0, others)], wbuf.at[pl.ds(0, others)], wsend).wait()
    for c in range(NCH):
        err_copy(c).wait()
    for copy in outs:
        copy.wait()
    keys_copy.wait()


def shards(features, key_grads, error_in, selected, bin_edges, threshold, moment, second, master):
    anywhere = pl.BlockSpec(memory_space=pl.ANY)
    vmem = pl.BlockSpec(memory_space=pltpu.VMEM)
    smem = pl.BlockSpec(memory_space=pltpu.SMEM)
    dma = pltpu.SemaphoreType.DMA
    state_shape = jax.ShapeDtypeStruct((REGION, HD), F32)
    return pl.pallas_call(
        kernel,
        out_shape=(
            jax.ShapeDtypeStruct((NZ * TOK, HD), BF16),
            jax.ShapeDtypeStruct((1, ROWS, HD), BF16),
            state_shape,
            state_shape,
            state_shape,
        ),
        in_specs=[anywhere, anywhere, anywhere, vmem, smem, smem, anywhere, anywhere, anywhere],
        out_specs=(anywhere,) * 5,
        scratch_shapes=[
            pltpu.VMEM((NZ, NCH, TOK, CW), BF16),
            pltpu.VMEM((NZ * TOK, HD), BF16),
            pltpu.VMEM((ROWS, HD), BF16),
            pltpu.VMEM((NCH, CW, HD), F32),
            pltpu.VMEM((NCH, CW, HD), F32),
            pltpu.VMEM((NCH, NBINS, CW), BF16),
            pltpu.VMEM((32, 1, HD), F32),
            pltpu.VMEM((NCH, CW, HD), BF16),
            pltpu.VMEM((NBINS, HD), F32),
            pltpu.VMEM((NDP, 8, HD), F32),
            pltpu.VMEM((NDP, 8, HD), F32),
            pltpu.VMEM((NDP, 1, HD), F32),
            pltpu.VMEM((NDP, REGION, HD), BF16),
            pltpu.VMEM((NZ * TOK, HD), F32),
            pltpu.VMEM((NZ * TOK, HD), BF16),
            pltpu.VMEM((3, REGION, HD), F32),
            pltpu.VMEM((3, REGION, HD), F32),
            dma((NCH,)),
            dma((8,)),
            dma((NCH,)),
            dma((2, 2)),
            dma((2, 4, NCH)),
            dma,
            dma,
            dma,
            dma,
            dma,
            dma((NY,)),
            dma((NX - 1, NY)),
            dma((NX, NY)),
        ],
        compiler_params=pltpu.CompilerParams(
            collective_id=0, has_side_effects=True, vmem_limit_bytes=48 * 1024 * 1024
        ),
        name="step",
    )(features, key_grads, error_in, selected, bin_edges, threshold, moment, second, master)


def solution(mesh):
    in_specs = (
        P(("dp", "tensor"), None),
        P("dp", "tensor"),
        P("dp", None, "tensor"),
        P("dp", "tensor", None),
        P(),
        P(),
        P("dp", "tensor"),
        P("dp", "tensor"),
        P("dp", "tensor"),
    )
    out_specs = (
        P("dp", "tensor"),
        P("dp", None, "tensor"),
        P("dp", "tensor"),
        P("dp", "tensor"),
        P("dp", "tensor"),
    )
    return jax.shard_map(shards, mesh=mesh, in_specs=in_specs, out_specs=out_specs, check_vma=False)
```

```python
import jax
import jax.numpy as jnp
from jax import lax
from jax.experimental import pallas as pl
from jax.experimental.pallas import tpu as pltpu
from jax.sharding import PartitionSpec as P

MESH = pl.DeviceIdType.MESH
F32 = jnp.float32
BF16 = jnp.bfloat16

ROWS = 4096
HD = 128
NZ = 8
NDP = 64
NX, NY = 4, 8
REGION = 64
TOK = 128
NCH = 8
CW = ROWS // NCH
NBINS = 16

beta_first = 0.9
beta_second = 0.95
learn_rate = 0.001
decay_rate = 0.1
epsilon = 1e-06
adam_epsilon = 1e-08
step_count = 10.0

NEAR_FIRST = (0, 1, 7, 2, 6, 3, 5, 4)


def dot(a, b):
    return lax.dot_general(a, b, (((1,), (0,)), ((), ())), preferred_element_type=F32)


def dot_t(a, b):
    return lax.dot_general(a, b, (((0,), (0,)), ((), ())), preferred_element_type=F32)


def split3(v):
    high = v.astype(BF16)
    rest = v - high.astype(F32)
    mid = rest.astype(BF16)
    low = (rest - mid.astype(F32)).astype(BF16)
    return high, mid, low


def kernel(
    feat, kg, err_in, sel_ref, edges, thr, mom, sec, mas,
    keys_out, err_out, mom_out, sec_out, mas_out,
    fbuf, gbuf, ein, acc, maskb, memb, vbuf, errb, ebins, tiles, got, eng, wbuf, kacc, kout, state, news,
    lsem, isem, osem, meet, zsend, zrecv, tsend, trecv, gsend, grecv, wsend, wa, wb, wc,
):
    z = lax.axis_index("tensor")
    me = lax.axis_index("dp")
    right, left = lax.rem(z + 1, NZ), lax.rem(z + NZ - 1, NZ)

    def load(c):
        return pltpu.make_async_copy(
            feat.at[:, pl.ds(pl.multiple_of(c * CW, CW), CW)], fbuf.at[z, c], lsem.at[c]
        )

    for c in range(NCH):
        load(c).start()
    loads = [
        pltpu.make_async_copy(kg, gbuf, isem.at[0]),
        pltpu.make_async_copy(err_in.at[0], ein, isem.at[1]),
        pltpu.make_async_copy(mom, state.at[0], isem.at[2]),
        pltpu.make_async_copy(sec, state.at[1], isem.at[3]),
        pltpu.make_async_copy(mas, state.at[2], isem.at[4]),
    ]
    for copy in loads:
        copy.start()

    barrier = pltpu.get_barrier_semaphore()
    x, y, core = me // (2 * NY), lax.rem(me // 2, NY), lax.rem(me, 2)
    partner = me + 1 - 2 * core

    def device(dx, dy, c):
        return (lax.rem(x + dx, NX) * NY + lax.rem(y + dy, NY)) * 2 + c

    along_x = (device(1, 0, core), device(NX - 1, 0, core))
    along_y = (device(0, 1, core), device(0, NY - 1, core))
    for near in (left, right):
        pl.semaphore_signal(barrier, inc=1, device_id={"tensor": near}, device_id_type=MESH)
    for near in (*along_x, *along_y, partner):
        pl.semaphore_signal(barrier, inc=1, device_id={"dp": near}, device_id_type=MESH)
    pl.semaphore_wait(barrier, 7)

    def hop(way, h, c, origin):
        return pltpu.make_async_remote_copy(
            src_ref=fbuf.at[origin, c],
            dst_ref=fbuf.at[origin, c],
            send_sem=zsend.at[way, 0 if h < 4 else 1],
            recv_sem=zrecv.at[way, h - 1, c],
            device_id={"tensor": right if way == 0 else left},
            device_id_type=MESH,
        )

    def first(c, carry):
        load(c).wait()
        hop(0, 1, c, z).start()
        hop(1, 1, c, z).start()
        return carry

    lax.fori_loop(0, NCH, first, 0)

    for turn, nears in enumerate((along_y, along_y, along_y, along_x, along_x, (partner,))):
        for near in nears:
            pl.semaphore_signal(meet.at[turn], inc=1, device_id={"dp": near}, device_id_type=MESH)
        pl.semaphore_wait(meet.at[turn], len(nears))

    sel = sel_ref[0]
    sub = lax.broadcasted_iota(jnp.int32, (HD, HD), 0)
    lane = lax.broadcasted_iota(jnp.int32, (HD, HD), 1)
    group_hot = jnp.where(sub[:32] == lax.shift_right_logical(sel, 7), 1.0, 0.0).astype(BF16)
    place_hot = jnp.where(sub == lax.bitwise_and(sel, 127), 1.0, 0.0).astype(BF16)
    chosen = lax.dot_general(
        group_hot, place_hot, (((1,), (1,)), ((), ())), preferred_element_type=F32
    )
    same = lax.shift_right_logical(sub, 6) == lax.shift_right_logical(lane, 6)
    before = jnp.where(same & (sub < lane), 1.0, 0.0).astype(BF16)
    rank = dot(chosen.astype(BF16), before)
    half = lax.shift_right_logical(lane[:32], 6).astype(F32) * 8.0
    slots = jnp.where(chosen > 0.5, half + rank, -1.0)
    for g in range(32):
        vbuf[g] = slots[g : g + 1]

    bin_of = lax.broadcasted_iota(jnp.int32, (NBINS, CW), 0)
    low_edge = jnp.zeros((NBINS, CW), jnp.int32)
    high_edge = jnp.zeros((NBINS, CW), jnp.int32)
    for b in range(NBINS):
        low_edge = jnp.where(bin_of == b, edges[b], low_edge)
        high_edge = jnp.where(bin_of == b, edges[b + 1], high_edge)
    row_of = lax.broadcasted_iota(jnp.int32, (NBINS, CW), 1)
    ones = jnp.ones((HD, HD), BF16)
    row_col = lax.broadcasted_iota(jnp.int32, (CW, HD), 0)

    for copy in loads[:2]:
        copy.wait()

    def shard_of(origin):
        return gbuf[pl.ds(pl.multiple_of(origin * TOK, TOK), TOK), :]

    def prepare(c, carry):
        rows = row_of + c * CW
        memb[c] = jnp.where((rows >= low_edge) & (rows < high_edge), 1.0, 0.0).astype(BF16)
        hit = jnp.where(row_col + c * CW == sel, 1.0, 0.0).astype(BF16)
        maskb[c] = dot(hit, ones)
        acc[c] = ein[pl.ds(pl.multiple_of(c * CW, CW), CW), :].astype(F32) + dot_t(
            fbuf[z, c], shard_of(z)
        )
        return carry

    lax.fori_loop(0, NCH, prepare, 0)
    ebins[...] = jnp.zeros_like(ebins)

    for h in (1, 2, 3):
        low = lax.rem(z + NZ - h, NZ)
        high = lax.rem(z + h, NZ)

        def step(c, carry, h=h, low=low, high=high):
            hop(0, h, c, low).wait_recv()
            if h < 3:
                hop(0, h + 1, c, low).start()
            else:

                @pl.when(c < NCH // 2)
                def _():
                    hop(0, 4, c, low).start()

            hop(1, h, c, high).wait_recv()
            if h < 3:
                hop(1, h + 1, c, high).start()
            else:

                @pl.when(c >= NCH // 2)
                def _():
                    hop(1, 4, c, high).start()

            acc[c] = acc[c] + (
                dot_t(fbuf[low, c], shard_of(low)) + dot_t(fbuf[high, c], shard_of(high))
            )
            return carry

        lax.fori_loop(0, NCH, step, 0)

    far = lax.rem(z + NZ // 2, NZ)
    sub16 = lax.broadcasted_iota(jnp.int32, (16, HD), 0)
    slot16 = sub16.astype(F32)
    map_line = lax.rem(sub16, 8) == 6

    def block_copy(owner):
        return pltpu.make_async_remote_copy(
            src_ref=tiles.at[owner],
            dst_ref=got.at[me],
            send_sem=tsend,
            recv_sem=trecv,
            device_id={"dp": owner},
            device_id_type=MESH,
        )

    def err_copy(c):
        return pltpu.make_async_copy(
            errb.at[c], err_out.at[0, pl.ds(pl.multiple_of(c * CW, CW), CW), :], osem.at[c]
        )

    def finish(c):
        total = acc[c] + dot_t(fbuf[far, c], shard_of(far))
        errb[c] = jnp.where(maskb[c] > 0.5, 0.0, total).astype(BF16)
        err_copy(c).start()
        square = total * total
        top = square.astype(BF16)
        rest = (square - top.astype(F32)).astype(BF16)
        ebins[...] += dot(memb[c], top) + dot(memb[c], rest)
        parts = split3(total)
        for g in range(4):
            line = vbuf[c * 4 + g]
            pick = jnp.where(slot16 == line, 1.0, 0.0).astype(BF16)
            picked = [dot(pick, part[g * HD : (g + 1) * HD]) for part in parts]
            tile = jnp.where(map_line, line, (picked[0] + picked[1]) + picked[2])
            tiles[pl.ds(c * 8 + 2 * g, 2)] = tile.reshape(2, 8, HD)
        for j in range(8):
            owner = c * 8 + j

            @pl.when(owner != me)
            def _():
                block_copy(owner).start()

            @pl.when(owner == me)
            def _():
                got[me] = tiles[owner]

    def last(i, carry):
        for way in (0, 1):
            c = i + way * (NCH // 2)
            hop(way, 4, c, far).wait_recv()
            finish(c)
        return carry

    lax.fori_loop(0, NCH // 2, last, 0)

    lane16 = lax.broadcasted_iota(jnp.int32, (NBINS, HD), 1)
    bin_sum = jnp.sum(ebins[...], axis=1, keepdims=True)
    eng[me] = jnp.sum(jnp.where(lane16 == sub16, bin_sum, 0.0), axis=0, keepdims=True)

    def energy_copy(k):
        return pltpu.make_async_remote_copy(
            src_ref=eng.at[me],
            dst_ref=eng.at[me],
            send_sem=gsend,
            recv_sem=grecv,
            device_id={"dp": lax.rem(me + k, NDP)},
            device_id_type=MESH,
        )

    def tell(k, carry):
        energy_copy(k).start()
        return carry

    lax.fori_loop(1, NDP, tell, 0)

    for copy in loads[2:]:
        copy.wait()
    others = NDP - 1
    pltpu.make_async_copy(got.at[pl.ds(0, others)], got.at[pl.ds(0, others)], trecv).wait()
    parity = lax.rem(me, 2)
    block = got[...]
    want = (lax.broadcasted_iota(jnp.int32, (NDP, 8, HD), 1) + 8 * parity).astype(F32)
    hot = jnp.where(want == block[:, 6:7, :], 1.0, 0.0).astype(BF16).reshape(NDP * 8, HD)
    parts = split3(block.reshape(NDP * 8, HD))
    both = (dot_t(hot, parts[0]) + dot_t(hot, parts[1])) + dot_t(hot, parts[2])
    kept_sum = both[:REGION] + both[REGION:]

    lane1 = lax.broadcasted_iota(jnp.int32, (1, HD), 1)
    low1 = jnp.zeros((1, HD), jnp.int32)
    high1 = jnp.zeros((1, HD), jnp.int32)
    for b in range(NBINS):
        low1 = jnp.where(lane1 == b, edges[b], low1)
        high1 = jnp.where(lane1 == b, edges[b + 1], high1)
    width = jnp.where(lane1 < NBINS, high1 - low1, 1).astype(F32)
    own_row = me * REGION + lax.broadcasted_iota(jnp.int32, (REGION, HD), 0)
    in_bin = (own_row >= low1) & (own_row < high1)

    pltpu.make_async_copy(eng.at[pl.ds(0, others)], eng.at[pl.ds(0, others)], grecv).wait()
    energy = jnp.sum(eng[...], axis=0)
    normal = 1.0 / jnp.sqrt(energy / (float(NDP * HD) * width) + epsilon)
    scale = jnp.where(lane1 >= thr[0], normal, 1.0)
    row_scale = jnp.sum(jnp.where(in_bin, scale, 0.0), axis=1, keepdims=True)
    grad = kept_sum * row_scale
    moment_new = beta_first * state[0] + (1.0 - beta_first) * grad
    second_new = beta_second * state[1] + (1.0 - beta_second) * grad * grad
    first_hat = moment_new / (1.0 - beta_first**step_count)
    second_hat = second_new / (1.0 - beta_second**step_count)
    master = state[2]
    master_new = master - learn_rate * (
        first_hat / (jnp.sqrt(second_hat) + adam_epsilon) + decay_rate * master
    )
    wbuf[me] = master_new.astype(BF16)

    def weight_copy(slot, to, sem):
        return pltpu.make_async_remote_copy(
            src_ref=wbuf.at[slot],
            dst_ref=wbuf.at[slot],
            send_sem=wsend,
            recv_sem=sem,
            device_id={"dp": to},
            device_id_type=MESH,
        )

    for k in NEAR_FIRST[1:]:
        weight_copy(me, device(0, k, core), wa.at[k]).start()
    news[0] = moment_new
    news[1] = second_new
    news[2] = master_new
    outs = [
        pltpu.make_async_copy(news.at[0], mom_out, isem.at[5]),
        pltpu.make_async_copy(news.at[1], sec_out, isem.at[6]),
        pltpu.make_async_copy(news.at[2], mas_out, isem.at[7]),
    ]
    for k in NEAR_FIRST:
        slot = device(0, NY - k, core)
        if k:
            weight_copy(slot, partner, wa.at[k]).wait_recv()
        for d in (1, 3, 2):
            weight_copy(slot, device(d, 0, core), wb.at[d - 1, k]).start()
        weight_copy(slot, partner, wc.at[0, k]).start()
    for copy in outs:
        copy.start()

    kacc[...] = jnp.zeros_like(kacc)

    def project(d):
        for k in NEAR_FIRST:
            weight_copy(device(NX - d, NY - k, 1 - core), partner, wc.at[d, k]).wait_recv()
        where_x = lax.rem(x + NX - d, NX)
        for part in range(2):
            c = where_x * 2 + part
            weight = wbuf[pl.ds(c * 8, 8)].reshape(CW, HD)
            kacc[...] += dot(fbuf[:, c].reshape(NZ * TOK, CW), weight)

    done = 0
    for d in (1, 3, 2):
        for k in NEAR_FIRST:
            slot = device(NX - d, NY - k, core)
            weight_copy(slot, partner, wb.at[d - 1, k]).wait_recv()
            weight_copy(slot, partner, wc.at[d, k]).start()
        project(done)
        done = d
    project(done)
    kout[...] = kacc[...].astype(BF16)
    keys_copy = pltpu.make_async_copy(kout, keys_out, isem.at[0])
    keys_copy.start()

    for way in (0, 1):
        pltpu.make_async_copy(
            fbuf.at[pl.ds(0, 3)], fbuf.at[pl.ds(0, 3)], zsend.at[way, 0]
        ).wait()
        pltpu.make_async_copy(
            fbuf.at[0, pl.ds(0, 4)], fbuf.at[0, pl.ds(0, 4)], zsend.at[way, 1]
        ).wait()
    pltpu.make_async_copy(got.at[pl.ds(0, others)], got.at[pl.ds(0, others)], tsend).wait()
    pltpu.make_async_copy(eng.at[pl.ds(0, others)], eng.at[pl.ds(0, others)], gsend).wait()
    pltpu.make_async_copy(wbuf.at[pl.ds(0, others)], wbuf.at[pl.ds(0, others)], wsend).wait()
    for c in range(NCH):
        err_copy(c).wait()
    for copy in outs:
        copy.wait()
    keys_copy.wait()


def put_out(
    keys, err, mom, sec, mas, keys_to, err_to, mom_to, sec_to, mas_to,
    keys_at, err_at, state_at, arrive, leave,
):
    quarter = ROWS // 4
    routes = []
    for q in range(4):
        rows = pl.ds(q * quarter, quarter)
        routes.append((err.at[0, rows, :], err_at.at[rows, :], err_to.at[0, rows, :]))
    routes.append((keys, keys_at, keys_to))
    for k, (a, b) in enumerate(((mom, mom_to), (sec, sec_to), (mas, mas_to))):
        routes.append((a, state_at.at[k], b))
    first = [pltpu.make_async_copy(a, b, arrive.at[k]) for k, (a, b, _) in enumerate(routes)]
    second = [pltpu.make_async_copy(b, c, leave.at[k]) for k, (_, b, c) in enumerate(routes)]
    for copy in first:
        copy.start()
    for one, two in zip(first, second):
        one.wait()
        two.start()
    for copy in second:
        copy.wait()


def shards(features, key_grads, error_in, selected, bin_edges, threshold, moment, second, master):
    hbm = pl.BlockSpec(memory_space=pltpu.HBM)
    vmem = pl.BlockSpec(memory_space=pltpu.VMEM)
    smem = pl.BlockSpec(memory_space=pltpu.SMEM)
    dma = pltpu.SemaphoreType.DMA
    state_shape = jax.ShapeDtypeStruct((REGION, HD), F32)
    out_shape = (
        jax.ShapeDtypeStruct((NZ * TOK, HD), BF16),
        jax.ShapeDtypeStruct((1, ROWS, HD), BF16),
        state_shape,
        state_shape,
        state_shape,
    )
    results = pl.pallas_call(
        kernel,
        out_shape=out_shape,
        in_specs=[hbm, hbm, hbm, vmem, smem, smem, hbm, hbm, hbm],
        out_specs=(hbm,) * 5,
        scratch_shapes=[
            pltpu.VMEM((NZ, NCH, TOK, CW), BF16),
            pltpu.VMEM((NZ * TOK, HD), BF16),
            pltpu.VMEM((ROWS, HD), BF16),
            pltpu.VMEM((NCH, CW, HD), F32),
            pltpu.VMEM((NCH, CW, HD), F32),
            pltpu.VMEM((NCH, NBINS, CW), BF16),
            pltpu.VMEM((32, 1, HD), F32),
            pltpu.VMEM((NCH, CW, HD), BF16),
            pltpu.VMEM((NBINS, HD), F32),
            pltpu.VMEM((NDP, 8, HD), F32),
            pltpu.VMEM((NDP, 8, HD), F32),
            pltpu.VMEM((NDP, 1, HD), F32),
            pltpu.VMEM((NDP, REGION, HD), BF16),
            pltpu.VMEM((NZ * TOK, HD), F32),
            pltpu.VMEM((NZ * TOK, HD), BF16),
            pltpu.VMEM((3, REGION, HD), F32),
            pltpu.VMEM((3, REGION, HD), F32),
            dma((NCH,)),
            dma((8,)),
            dma((NCH,)),
            pltpu.SemaphoreType.REGULAR((6,)),
            dma((2, 2)),
            dma((2, 4, NCH)),
            dma,
            dma,
            dma,
            dma,
            dma,
            dma((NY,)),
            dma((NX - 1, NY)),
            dma((NX, NY)),
        ],
        compiler_params=pltpu.CompilerParams(
            collective_id=0, has_side_effects=True, vmem_limit_bytes=58 * 1024 * 1024
        ),
        name="step",
    )(features, key_grads, error_in, selected, bin_edges, threshold, moment, second, master)
    return pl.pallas_call(
        put_out,
        out_shape=out_shape,
        in_specs=[hbm] * 5,
        out_specs=(hbm,) * 5,
        scratch_shapes=[
            pltpu.VMEM((NZ * TOK, HD), BF16),
            pltpu.VMEM((ROWS, HD), BF16),
            pltpu.VMEM((3, REGION, HD), F32),
            dma((8,)),
            dma((8,)),
        ],
        compiler_params=pltpu.CompilerParams(vmem_limit_bytes=58 * 1024 * 1024),
        name="put_out",
    )(*results)


def solution(mesh):
    in_specs = (
        P(("dp", "tensor"), None),
        P("dp", "tensor"),
        P("dp", None, "tensor"),
        P("dp", "tensor", None),
        P(),
        P(),
        P("dp", "tensor"),
        P("dp", "tensor"),
        P("dp", "tensor"),
    )
    out_specs = (
        P("dp", "tensor"),
        P("dp", None, "tensor"),
        P("dp", "tensor"),
        P("dp", "tensor"),
        P("dp", "tensor"),
    )
    return jax.shard_map(shards, mesh=mesh, in_specs=in_specs, out_specs=out_specs, check_vma=False)
```

```python
import jax
import jax.numpy as jnp
from jax import lax
from jax.experimental import pallas as pl
from jax.experimental.pallas import tpu as pltpu
from jax.sharding import PartitionSpec as P

MESH = pl.DeviceIdType.MESH
F32 = jnp.float32
BF16 = jnp.bfloat16

ROWS = 4096
HD = 128
NZ = 8
NDP = 64
NX, NY = 4, 8
REGION = 64
TOK = 128
NCH = 16
HALF = NCH // 2
CW = ROWS // NCH
OWNERS = CW // REGION
NBINS = 16

beta_first = 0.9
beta_second = 0.95
learn_rate = 0.001
decay_rate = 0.1
epsilon = 1e-06
adam_epsilon = 1e-08
step_count = 10.0

NEAR_FIRST = (0, 1, 7, 2, 6, 3, 5, 4)
FAR_FIRST_Y = (4, 3, 5, 2, 6, 1, 7, 0)
FAR_FIRST_X = (2, 1, 3, 0)


def dot(a, b):
    return lax.dot_general(a, b, (((1,), (0,)), ((), ())), preferred_element_type=F32)


def dot_t(a, b):
    return lax.dot_general(a, b, (((0,), (0,)), ((), ())), preferred_element_type=F32)


def split3(v):
    high = v.astype(BF16)
    rest = v - high.astype(F32)
    mid = rest.astype(BF16)
    low = (rest - mid.astype(F32)).astype(BF16)
    return high, mid, low


def kernel(
    feat, kg, err_in, sel_ref, edges, thr, mom, sec, mas,
    keys_out, err_out, mom_out, sec_out, mas_out,
    fbuf, gbuf, ein, acc, maskb, memb, vbuf, errb, ebins, tiles, got, eng, wbuf, kacc, kout, state, news,
    lsem, isem, osem, meet, zsend, zrecv, tsend, trecv, gsend, grecv, wsend, wa, wb, wc,
):
    z = lax.axis_index("tensor")
    me = lax.axis_index("dp")
    right, left = lax.rem(z + 1, NZ), lax.rem(z + NZ - 1, NZ)

    barrier = pltpu.get_barrier_semaphore()
    x, y, core = me // (2 * NY), lax.rem(me // 2, NY), lax.rem(me, 2)
    partner = me + 1 - 2 * core

    at_x = [lax.rem(x + d, NX) * (2 * NY) for d in range(NX)]
    at_y = [lax.rem(y + d, NY) * 2 for d in range(NY)]

    def device(dx, dy, c):
        return at_x[dx % NX] + at_y[dy % NY] + c

    along_x = (device(1, 0, core), device(NX - 1, 0, core))
    along_y = (device(0, 1, core), device(0, NY - 1, core))
    for near in (left, right):
        pl.semaphore_signal(barrier, inc=1, device_id={"tensor": near}, device_id_type=MESH)
    for near in (*along_x, *along_y, partner):
        pl.semaphore_signal(barrier, inc=1, device_id={"dp": near}, device_id_type=MESH)

    def load(c):
        return pltpu.make_async_copy(
            feat.at[:, pl.ds(pl.multiple_of(c * CW, CW), CW)], fbuf.at[z, c], lsem.at[c]
        )

    pl.semaphore_wait(barrier, 7)

    def hop(way, h, c, origin):
        return pltpu.make_async_remote_copy(
            src_ref=fbuf.at[origin, c],
            dst_ref=fbuf.at[origin, c],
            send_sem=zsend.at[way, 0 if h < 4 else 1],
            recv_sem=zrecv.at[way, h - 1, c],
            device_id={"tensor": right if way == 0 else left},
            device_id_type=MESH,
        )

    def first(i, carry):
        for way in (0, 1):
            c = lax.rem(i + way * HALF, NCH)
            pltpu.make_async_remote_copy(
                src_ref=feat.at[:, pl.ds(pl.multiple_of(c * CW, CW), CW)],
                dst_ref=fbuf.at[z, c],
                send_sem=zsend.at[way, 0],
                recv_sem=zrecv.at[way, 0, c],
                device_id={"tensor": right if way == 0 else left},
                device_id_type=MESH,
            ).start()
        return carry

    lax.fori_loop(0, NCH, first, 0)

    for i in range(HALF):
        load(i).start()
        load(i + HALF).start()
    loads = [
        pltpu.make_async_copy(kg, gbuf, isem.at[0]),
        pltpu.make_async_copy(err_in.at[0], ein, isem.at[1]),
        pltpu.make_async_copy(mom, state.at[0], isem.at[2]),
        pltpu.make_async_copy(sec, state.at[1], isem.at[3]),
        pltpu.make_async_copy(mas, state.at[2], isem.at[4]),
    ]
    for copy in loads:
        copy.start()

    for turn, nears in enumerate((along_y, along_y, along_y, along_x, along_x, (partner,))):
        for near in nears:
            pl.semaphore_signal(meet.at[turn], inc=1, device_id={"dp": near}, device_id_type=MESH)
        pl.semaphore_wait(meet.at[turn], len(nears))

    sel = sel_ref[0]
    sub = lax.broadcasted_iota(jnp.int32, (HD, HD), 0)
    lane = lax.broadcasted_iota(jnp.int32, (HD, HD), 1)
    group_hot = jnp.where(sub[:32] == lax.shift_right_logical(sel, 7), 1.0, 0.0).astype(BF16)
    place_hot = jnp.where(sub == lax.bitwise_and(sel, 127), 1.0, 0.0).astype(BF16)
    chosen = lax.dot_general(
        group_hot, place_hot, (((1,), (1,)), ((), ())), preferred_element_type=F32
    )
    same = lax.shift_right_logical(sub, 6) == lax.shift_right_logical(lane, 6)
    before = jnp.where(same & (sub < lane), 1.0, 0.0).astype(BF16)
    rank = dot(chosen.astype(BF16), before)
    half = lax.shift_right_logical(lane[:32], 6).astype(F32) * 8.0
    slots = jnp.where(chosen > 0.5, half + rank, -1.0)
    for g in range(32):
        vbuf[g] = slots[g : g + 1]

    bin_of = lax.broadcasted_iota(jnp.int32, (NBINS, CW), 0)
    low_edge = jnp.zeros((NBINS, CW), jnp.int32)
    high_edge = jnp.zeros((NBINS, CW), jnp.int32)
    for b in range(NBINS):
        low_edge = jnp.where(bin_of == b, edges[b], low_edge)
        high_edge = jnp.where(bin_of == b, edges[b + 1], high_edge)
    row_of = lax.broadcasted_iota(jnp.int32, (NBINS, CW), 1)
    ones = jnp.ones((HD, HD), BF16)
    row_col = lax.broadcasted_iota(jnp.int32, (CW, HD), 0)

    for copy in loads[:2]:
        copy.wait()

    def shard_of(origin):
        return gbuf[pl.ds(pl.multiple_of(origin * TOK, TOK), TOK), :]

    def prepare(c, carry):
        load(c).wait()
        rows = row_of + c * CW
        memb[c] = jnp.where((rows >= low_edge) & (rows < high_edge), 1.0, 0.0).astype(BF16)
        hit = jnp.where(row_col + c * CW == sel, 1.0, 0.0).astype(BF16)
        maskb[c] = dot(hit, ones)
        acc[c] = ein[pl.ds(pl.multiple_of(c * CW, CW), CW), :].astype(F32) + dot_t(
            fbuf[z, c], shard_of(z)
        )
        return carry

    lax.fori_loop(0, NCH, prepare, 0)
    ebins[...] = jnp.zeros_like(ebins)

    lows = [lax.rem(z + NZ - h, NZ) for h in range(4)]
    highs = [lax.rem(z + h, NZ) for h in range(4)]

    def places(i):
        return (i, lax.rem(i + HALF, NCH))

    def take(h, i):
        for way, origin in ((0, lows[h]), (1, highs[h])):
            c = places(i)[way]
            acc[c] = acc[c] + dot_t(fbuf[origin, c], shard_of(origin))

    def step1(i, carry):
        for way, origin in ((0, lows[1]), (1, highs[1])):
            hop(way, 1, places(i)[way], origin).wait_recv()
            hop(way, 2, places(i)[way], origin).start()
        take(1, i)
        return carry

    def step2(i, carry):
        for way, origin in ((0, lows[2]), (1, highs[2])):
            hop(way, 2, places(i)[way], origin).wait_recv()

            @pl.when(i < HALF)
            def _():
                hop(way, 3, places(i)[way], origin).start()

        take(2, i)
        return carry

    def step3(i, carry):
        for way in (0, 1):
            hop(way, 3, places(i)[way], (lows[3], highs[3])[way]).wait_recv()
            hop(way, 3, places(i + HALF)[way], (lows[2], highs[2])[way]).start()
            hop(way, 4, places(i)[way], (lows[3], highs[3])[way]).start()
        take(3, i)
        return carry

    lax.fori_loop(0, NCH, step1, 0)
    lax.fori_loop(0, NCH, step2, 0)
    lax.fori_loop(0, HALF, step3, 0)

    far = lax.rem(z + NZ // 2, NZ)
    sub16 = lax.broadcasted_iota(jnp.int32, (16, HD), 0)
    slot16 = sub16.astype(F32)
    map_line = lax.rem(sub16, 8) == 6

    def block_copy(owner):
        return pltpu.make_async_remote_copy(
            src_ref=tiles.at[owner],
            dst_ref=got.at[me],
            send_sem=tsend,
            recv_sem=trecv,
            device_id={"dp": owner},
            device_id_type=MESH,
        )

    def err_copy(c):
        return pltpu.make_async_copy(
            errb.at[c], err_out.at[0, pl.ds(pl.multiple_of(c * CW, CW), CW), :], osem.at[c]
        )

    def finish(c):
        total = acc[c] + dot_t(fbuf[far, c], shard_of(far))
        acc[c] = total
        square = total * total
        top = square.astype(BF16)
        rest = (square - top.astype(F32)).astype(BF16)
        ebins[...] += dot(memb[c], top) + dot(memb[c], rest)
        parts = split3(total)
        for g in range(CW // HD):
            line = vbuf[c * (CW // HD) + g]
            pick = jnp.where(slot16 == line, 1.0, 0.0).astype(BF16)
            picked = [dot(pick, part[g * HD : (g + 1) * HD]) for part in parts]
            tile = jnp.where(map_line, line, (picked[0] + picked[1]) + picked[2])
            tiles[pl.ds(c * OWNERS + 2 * g, 2)] = tile.reshape(2, 8, HD)
        for j in range(OWNERS):
            owner = c * OWNERS + j

            @pl.when(owner != me)
            def _():
                block_copy(owner).start()

            @pl.when(owner == me)
            def _():
                got[me] = tiles[owner]

    def last(i, carry):
        for way in (0, 1):
            hop(way, 3, places(i + HALF)[way], (lows[3], highs[3])[way]).wait_recv()
        take(3, i + HALF)
        for way in (0, 1):
            c = i + way * HALF
            hop(way, 4, c, far).wait_recv()
            finish(c)
        return carry

    lax.fori_loop(0, HALF, last, 0)

    lane16 = lax.broadcasted_iota(jnp.int32, (NBINS, HD), 1)
    bin_sum = jnp.sum(ebins[...], axis=1, keepdims=True)
    eng[me] = jnp.sum(jnp.where(lane16 == sub16, bin_sum, 0.0), axis=0, keepdims=True)

    for dy in FAR_FIRST_Y:
        for dx in FAR_FIRST_X:
            for dc in (1, 0):
                if dx or dy or dc:
                    pltpu.make_async_remote_copy(
                        src_ref=eng.at[me],
                        dst_ref=eng.at[me],
                        send_sem=gsend,
                        recv_sem=grecv,
                        device_id={"dp": device(dx, dy, 1 - core if dc else core)},
                        device_id_type=MESH,
                    ).start()

    def residual(c, carry):
        errb[c] = jnp.where(maskb[c] > 0.5, 0.0, acc[c]).astype(BF16)
        err_copy(c).start()
        return carry

    lax.fori_loop(0, NCH, residual, 0)

    for copy in loads[2:]:
        copy.wait()
    others = NDP - 1
    pltpu.make_async_copy(got.at[pl.ds(0, others)], got.at[pl.ds(0, others)], trecv).wait()
    parity = lax.rem(me, 2)
    block = got[...]
    want = (lax.broadcasted_iota(jnp.int32, (NDP, 8, HD), 1) + 8 * parity).astype(F32)
    hot = jnp.where(want == block[:, 6:7, :], 1.0, 0.0).astype(BF16).reshape(NDP * 8, HD)
    parts = split3(block.reshape(NDP * 8, HD))
    both = (dot_t(hot, parts[0]) + dot_t(hot, parts[1])) + dot_t(hot, parts[2])
    kept_sum = both[:REGION] + both[REGION:]

    lane1 = lax.broadcasted_iota(jnp.int32, (1, HD), 1)
    low1 = jnp.zeros((1, HD), jnp.int32)
    high1 = jnp.zeros((1, HD), jnp.int32)
    for b in range(NBINS):
        low1 = jnp.where(lane1 == b, edges[b], low1)
        high1 = jnp.where(lane1 == b, edges[b + 1], high1)
    width = jnp.where(lane1 < NBINS, high1 - low1, 1).astype(F32)
    own_row = me * REGION + lax.broadcasted_iota(jnp.int32, (REGION, HD), 0)
    in_bin = (own_row >= low1) & (own_row < high1)

    pltpu.make_async_copy(eng.at[pl.ds(0, others)], eng.at[pl.ds(0, others)], grecv).wait()
    energy = jnp.sum(eng[...], axis=0)
    normal = 1.0 / jnp.sqrt(energy / (float(NDP * HD) * width) + epsilon)
    scale = jnp.where(lane1 >= thr[...], normal, 1.0)
    row_scale = jnp.sum(jnp.where(in_bin, scale, 0.0), axis=1, keepdims=True)
    grad = kept_sum * row_scale
    moment_new = beta_first * state[0] + (1.0 - beta_first) * grad
    second_new = beta_second * state[1] + (1.0 - beta_second) * grad * grad
    first_hat = moment_new / (1.0 - beta_first**step_count)
    second_hat = second_new / (1.0 - beta_second**step_count)
    master = state[2]
    master_new = master - learn_rate * (
        first_hat / (jnp.sqrt(second_hat) + adam_epsilon) + decay_rate * master
    )
    wbuf[me] = master_new.astype(BF16)

    def weight_copy(slot, to, sem):
        return pltpu.make_async_remote_copy(
            src_ref=wbuf.at[slot],
            dst_ref=wbuf.at[slot],
            send_sem=wsend,
            recv_sem=sem,
            device_id={"dp": to},
            device_id_type=MESH,
        )

    for k in NEAR_FIRST[1:]:
        weight_copy(me, device(0, k, core), wa.at[k]).start()
    news[0] = moment_new
    news[1] = second_new
    news[2] = master_new
    outs = [
        pltpu.make_async_copy(news.at[0], mom_out, isem.at[5]),
        pltpu.make_async_copy(news.at[1], sec_out, isem.at[6]),
        pltpu.make_async_copy(news.at[2], mas_out, isem.at[7]),
    ]
    for k in NEAR_FIRST:
        slot = device(0, NY - k, core)
        if k:
            weight_copy(slot, partner, wa.at[k]).wait_recv()
        for d in (1, 3, 2):
            weight_copy(slot, device(d, 0, core), wb.at[d - 1, k]).start()
        weight_copy(slot, partner, wc.at[0, k]).start()
    for copy in outs:
        copy.start()

    def pass_on(d):
        for k in NEAR_FIRST:
            slot = device(NX - d, NY - k, core)
            weight_copy(slot, partner, wb.at[d - 1, k]).wait_recv()
            weight_copy(slot, partner, wc.at[d, k]).start()

    def share(d):
        for k in NEAR_FIRST:
            weight_copy(device(NX - d, NY - k, 1 - core), partner, wc.at[d, k]).wait_recv()
        where_x = lax.rem(x + NX - d, NX)
        total = None
        for part in range(NY // 2):
            c = where_x * (NY // 2) + part
            weight = wbuf[pl.ds(c * OWNERS, OWNERS)].reshape(CW, HD)
            one = dot(fbuf[:, c].reshape(NZ * TOK, CW), weight)
            total = one if total is None else total + one
        return total

    pass_on(1)
    pass_on(3)
    kacc[...] = share(0)
    pass_on(2)
    kacc[...] += share(1)
    kacc[...] += share(3)
    kout[...] = (kacc[...] + share(2)).astype(BF16)
    keys_copy = pltpu.make_async_copy(kout, keys_out, isem.at[0])
    keys_copy.start()

    for way in (0, 1):
        pltpu.make_async_copy(
            fbuf.at[pl.ds(0, 3)], fbuf.at[pl.ds(0, 3)], zsend.at[way, 0]
        ).wait()
        pltpu.make_async_copy(
            fbuf.at[0, pl.ds(0, HALF)], fbuf.at[0, pl.ds(0, HALF)], zsend.at[way, 1]
        ).wait()
    pltpu.make_async_copy(got.at[pl.ds(0, others)], got.at[pl.ds(0, others)], tsend).wait()
    pltpu.make_async_copy(eng.at[pl.ds(0, others)], eng.at[pl.ds(0, others)], gsend).wait()
    pltpu.make_async_copy(wbuf.at[pl.ds(0, others)], wbuf.at[pl.ds(0, others)], wsend).wait()
    for c in range(NCH):
        err_copy(c).wait()
    for copy in outs:
        copy.wait()
    keys_copy.wait()


def put_out(
    keys, err, mom, sec, mas, keys_to, err_to, mom_to, sec_to, mas_to,
    keys_at, err_at, state_at, arrive, leave,
):
    eighth = ROWS // 8
    routes = []
    for q in range(8):
        rows = pl.ds(q * eighth, eighth)
        routes.append((err.at[0, rows, :], err_at.at[rows, :], err_to.at[0, rows, :]))
    routes.append((keys, keys_at, keys_to))
    for k, (a, b) in enumerate(((mom, mom_to), (sec, sec_to), (mas, mas_to))):
        routes.append((a, state_at.at[k], b))
    first = [pltpu.make_async_copy(a, b, arrive.at[k]) for k, (a, b, _) in enumerate(routes)]
    second = [pltpu.make_async_copy(b, c, leave.at[k]) for k, (_, b, c) in enumerate(routes)]
    for copy in first:
        copy.start()
    for one, two in zip(first, second):
        one.wait()
        two.start()
    for copy in second:
        copy.wait()


def shards(features, key_grads, error_in, selected, bin_edges, threshold, moment, second, master):
    hbm = pl.BlockSpec(memory_space=pltpu.HBM)
    vmem = pl.BlockSpec(memory_space=pltpu.VMEM)
    smem = pl.BlockSpec(memory_space=pltpu.SMEM)
    dma = pltpu.SemaphoreType.DMA
    state_shape = jax.ShapeDtypeStruct((REGION, HD), F32)
    out_shape = (
        jax.ShapeDtypeStruct((NZ * TOK, HD), BF16),
        jax.ShapeDtypeStruct((1, ROWS, HD), BF16),
        state_shape,
        state_shape,
        state_shape,
    )
    results = pl.pallas_call(
        kernel,
        out_shape=out_shape,
        in_specs=[hbm, hbm, hbm, vmem, smem, vmem, hbm, hbm, hbm],
        out_specs=(hbm,) * 5,
        scratch_shapes=[
            pltpu.VMEM((NZ, NCH, TOK, CW), BF16),
            pltpu.VMEM((NZ * TOK, HD), BF16),
            pltpu.VMEM((ROWS, HD), BF16),
            pltpu.VMEM((NCH, CW, HD), F32),
            pltpu.VMEM((NCH, CW, HD), F32),
            pltpu.VMEM((NCH, NBINS, CW), BF16),
            pltpu.VMEM((32, 1, HD), F32),
            pltpu.VMEM((NCH, CW, HD), BF16),
            pltpu.VMEM((NBINS, HD), F32),
            pltpu.VMEM((NDP, 8, HD), F32),
            pltpu.VMEM((NDP, 8, HD), F32),
            pltpu.VMEM((NDP, 1, HD), F32),
            pltpu.VMEM((NDP, REGION, HD), BF16),
            pltpu.VMEM((NZ * TOK, HD), F32),
            pltpu.VMEM((NZ * TOK, HD), BF16),
            pltpu.VMEM((3, REGION, HD), F32),
            pltpu.VMEM((3, REGION, HD), F32),
            dma((NCH,)),
            dma((8,)),
            dma((NCH,)),
            pltpu.SemaphoreType.REGULAR((6,)),
            dma((2, 2)),
            dma((2, 4, NCH)),
            dma,
            dma,
            dma,
            dma,
            dma,
            dma((NY,)),
            dma((NX - 1, NY)),
            dma((NX, NY)),
        ],
        compiler_params=pltpu.CompilerParams(
            collective_id=0, has_side_effects=True, vmem_limit_bytes=58 * 1024 * 1024
        ),
        name="step",
    )(features, key_grads, error_in, selected, bin_edges, threshold.reshape(1, 1), moment, second, master)
    return pl.pallas_call(
        put_out,
        out_shape=out_shape,
        in_specs=[hbm] * 5,
        out_specs=(hbm,) * 5,
        scratch_shapes=[
            pltpu.VMEM((NZ * TOK, HD), BF16),
            pltpu.VMEM((ROWS, HD), BF16),
            pltpu.VMEM((3, REGION, HD), F32),
            dma((12,)),
            dma((12,)),
        ],
        compiler_params=pltpu.CompilerParams(vmem_limit_bytes=58 * 1024 * 1024),
        name="put_out",
    )(*results)


def solution(mesh):
    in_specs = (
        P(("dp", "tensor"), None),
        P("dp", "tensor"),
        P("dp", None, "tensor"),
        P("dp", "tensor", None),
        P(),
        P(),
        P("dp", "tensor"),
        P("dp", "tensor"),
        P("dp", "tensor"),
    )
    out_specs = (
        P("dp", "tensor"),
        P("dp", None, "tensor"),
        P("dp", "tensor"),
        P("dp", "tensor"),
        P("dp", "tensor"),
    )
    return jax.shard_map(shards, mesh=mesh, in_specs=in_specs, out_specs=out_specs, check_vma=False)
```

```python
import jax
import jax.numpy as jnp
from jax import lax
from jax.experimental import pallas as pl
from jax.experimental.pallas import tpu as pltpu
from jax.sharding import PartitionSpec as P

MESH = pl.DeviceIdType.MESH
F32 = jnp.float32
BF16 = jnp.bfloat16

ROWS = 4096
HD = 128
NZ = 8
NDP = 64
NX, NY = 4, 8
REGION = 64
TOK = 128
NCH = 16
HALF = NCH // 2
CW = ROWS // NCH
OWNERS = CW // REGION
NBINS = 16

beta_first = 0.9
beta_second = 0.95
learn_rate = 0.001
decay_rate = 0.1
epsilon = 1e-06
adam_epsilon = 1e-08
step_count = 10.0

NEAR_FIRST = (0, 1, 7, 2, 6, 3, 5, 4)
FAR_FIRST_Y = (4, 3, 5, 2, 6, 1, 7, 0)
FAR_FIRST_X = (2, 1, 3, 0)


def dot(a, b):
    return lax.dot_general(a, b, (((1,), (0,)), ((), ())), preferred_element_type=F32)


def dot_t(a, b):
    return lax.dot_general(a, b, (((0,), (0,)), ((), ())), preferred_element_type=F32)


def split3(v):
    high = v.astype(BF16)
    rest = v - high.astype(F32)
    mid = rest.astype(BF16)
    low = (rest - mid.astype(F32)).astype(BF16)
    return high, mid, low


def kernel(
    feat, kg, err_in, sel_ref, edges, thr, mom, sec, mas,
    keys_out, err_out, mom_out, sec_out, mas_out,
    fbuf, gbuf, ein, acc, maskb, memb, vbuf, errb, ebins, tiles, got, eng, wbuf, kacc, kout, state, news,
    lsem, isem, osem, meet, zsend, zrecv, tsend, trecv, gsend, grecv, wsend, wa, wb, wc,
):
    z = lax.axis_index("tensor")
    me = lax.axis_index("dp")
    right, left = lax.rem(z + 1, NZ), lax.rem(z + NZ - 1, NZ)

    barrier = pltpu.get_barrier_semaphore()
    x, y, core = me // (2 * NY), lax.rem(me // 2, NY), lax.rem(me, 2)
    partner = me + 1 - 2 * core

    at_x = [lax.rem(x + d, NX) * (2 * NY) for d in range(NX)]
    at_y = [lax.rem(y + d, NY) * 2 for d in range(NY)]

    def device(dx, dy, c):
        return at_x[dx % NX] + at_y[dy % NY] + c

    along_x = (device(1, 0, core), device(NX - 1, 0, core))
    along_y = (device(0, 1, core), device(0, NY - 1, core))
    for near in (left, right):
        pl.semaphore_signal(barrier, inc=1, device_id={"tensor": near}, device_id_type=MESH)
    for near in (*along_x, *along_y, partner):
        pl.semaphore_signal(barrier, inc=1, device_id={"dp": near}, device_id_type=MESH)

    def load(c):
        return pltpu.make_async_copy(
            feat.at[:, pl.ds(pl.multiple_of(c * CW, CW), CW)], fbuf.at[z, c], lsem.at[c]
        )

    pl.semaphore_wait(barrier, 7)

    def hop(way, h, c, origin):
        return pltpu.make_async_remote_copy(
            src_ref=fbuf.at[origin, c],
            dst_ref=fbuf.at[origin, c],
            send_sem=zsend.at[way, 0 if h < 4 else 1],
            recv_sem=zrecv.at[way, h - 1, c],
            device_id={"tensor": right if way == 0 else left},
            device_id_type=MESH,
        )

    def first(i, carry):
        for way in (0, 1):
            c = lax.rem(i + way * HALF, NCH)
            pltpu.make_async_remote_copy(
                src_ref=feat.at[:, pl.ds(pl.multiple_of(c * CW, CW), CW)],
                dst_ref=fbuf.at[z, c],
                send_sem=zsend.at[way, 0],
                recv_sem=zrecv.at[way, 0, c],
                device_id={"tensor": right if way == 0 else left},
                device_id_type=MESH,
            ).start()
        return carry

    lax.fori_loop(0, NCH, first, 0)

    for i in range(HALF):
        load(i).start()
        load(i + HALF).start()
    loads = [
        pltpu.make_async_copy(kg, gbuf, isem.at[0]),
        pltpu.make_async_copy(err_in.at[0], ein, isem.at[1]),
        pltpu.make_async_copy(mom, state.at[0], isem.at[2]),
        pltpu.make_async_copy(sec, state.at[1], isem.at[3]),
        pltpu.make_async_copy(mas, state.at[2], isem.at[4]),
    ]
    for copy in loads:
        copy.start()

    for turn, nears in enumerate((along_y, along_y, along_y, along_x, along_x, (partner,))):
        for near in nears:
            pl.semaphore_signal(meet.at[turn], inc=1, device_id={"dp": near}, device_id_type=MESH)
        pl.semaphore_wait(meet.at[turn], len(nears))

    sel = sel_ref[0]
    sub = lax.broadcasted_iota(jnp.int32, (HD, HD), 0)
    lane = lax.broadcasted_iota(jnp.int32, (HD, HD), 1)
    group_hot = jnp.where(sub[:32] == lax.shift_right_logical(sel, 7), 1.0, 0.0).astype(BF16)
    place_hot = jnp.where(sub == lax.bitwise_and(sel, 127), 1.0, 0.0).astype(BF16)
    chosen = lax.dot_general(
        group_hot, place_hot, (((1,), (1,)), ((), ())), preferred_element_type=F32
    )
    same = lax.shift_right_logical(sub, 6) == lax.shift_right_logical(lane, 6)
    before = jnp.where(same & (sub < lane), 1.0, 0.0).astype(BF16)
    rank = dot(chosen.astype(BF16), before)
    half = lax.shift_right_logical(lane[:32], 6).astype(F32) * 8.0
    slots = jnp.where(chosen > 0.5, half + rank, -1.0)
    for g in range(32):
        vbuf[g] = slots[g : g + 1]

    bin_of = lax.broadcasted_iota(jnp.int32, (NBINS, CW), 0)
    low_edge = jnp.zeros((NBINS, CW), jnp.int32)
    high_edge = jnp.zeros((NBINS, CW), jnp.int32)
    for b in range(NBINS):
        low_edge = jnp.where(bin_of == b, edges[b], low_edge)
        high_edge = jnp.where(bin_of == b, edges[b + 1], high_edge)
    row_of = lax.broadcasted_iota(jnp.int32, (NBINS, CW), 1)
    ones = jnp.ones((HD, HD), BF16)
    row_col = lax.broadcasted_iota(jnp.int32, (CW, HD), 0)

    for copy in loads[:2]:
        copy.wait()

    def shard_of(origin):
        return gbuf[pl.ds(pl.multiple_of(origin * TOK, TOK), TOK), :]

    def prepare(c, carry):
        load(c).wait()
        rows = row_of + c * CW
        memb[c] = jnp.where((rows >= low_edge) & (rows < high_edge), 1.0, 0.0).astype(BF16)
        hit = jnp.where(row_col + c * CW == sel, 1.0, 0.0).astype(BF16)
        maskb[c] = dot(hit, ones)
        acc[c] = ein[pl.ds(pl.multiple_of(c * CW, CW), CW), :].astype(F32) + dot_t(
            fbuf[z, c], shard_of(z)
        )
        return carry

    lax.fori_loop(0, NCH, prepare, 0)
    ebins[...] = jnp.zeros_like(ebins)

    lows = [lax.rem(z + NZ - h, NZ) for h in range(4)]
    highs = [lax.rem(z + h, NZ) for h in range(4)]

    def places(i):
        return (i, lax.rem(i + HALF, NCH))

    def take(h, i):
        for way, origin in ((0, lows[h]), (1, highs[h])):
            c = places(i)[way]
            acc[c] = acc[c] + dot_t(fbuf[origin, c], shard_of(origin))

    def step1(i, carry):
        for way, origin in ((0, lows[1]), (1, highs[1])):
            hop(way, 1, places(i)[way], origin).wait_recv()
            hop(way, 2, places(i)[way], origin).start()
        take(1, i)
        return carry

    def step2(i, carry):
        for way, origin in ((0, lows[2]), (1, highs[2])):
            hop(way, 2, places(i)[way], origin).wait_recv()

            @pl.when(i < HALF)
            def _():
                hop(way, 3, places(i)[way], origin).start()

        take(2, i)
        return carry

    def step3(i, carry):
        for way in (0, 1):
            hop(way, 3, places(i)[way], (lows[3], highs[3])[way]).wait_recv()
            hop(way, 3, places(i + HALF)[way], (lows[2], highs[2])[way]).start()
            hop(way, 4, places(i)[way], (lows[3], highs[3])[way]).start()
        take(3, i)
        return carry

    lax.fori_loop(0, NCH, step1, 0)
    lax.fori_loop(0, NCH, step2, 0)
    lax.fori_loop(0, HALF, step3, 0)

    far = lax.rem(z + NZ // 2, NZ)
    sub16 = lax.broadcasted_iota(jnp.int32, (16, HD), 0)
    slot16 = sub16.astype(F32)
    map_line = lax.rem(sub16, 8) == 6

    def block_copy(owner):
        return pltpu.make_async_remote_copy(
            src_ref=tiles.at[owner],
            dst_ref=got.at[me],
            send_sem=tsend,
            recv_sem=trecv,
            device_id={"dp": owner},
            device_id_type=MESH,
        )

    def err_copy(c):
        return pltpu.make_async_copy(
            errb.at[c], err_out.at[0, pl.ds(pl.multiple_of(c * CW, CW), CW), :], osem.at[c]
        )

    def finish(c):
        total = acc[c] + dot_t(fbuf[far, c], shard_of(far))
        acc[c] = total
        square = total * total
        top = square.astype(BF16)
        rest = (square - top.astype(F32)).astype(BF16)
        ebins[...] += dot(memb[c], top) + dot(memb[c], rest)
        parts = split3(total)
        for g in range(CW // HD):
            line = vbuf[c * (CW // HD) + g]
            pick = jnp.where(slot16 == line, 1.0, 0.0).astype(BF16)
            picked = [dot(pick, part[g * HD : (g + 1) * HD]) for part in parts]
            tile = jnp.where(map_line, line, (picked[0] + picked[1]) + picked[2])
            tiles[pl.ds(c * OWNERS + 2 * g, 2)] = tile.reshape(2, 8, HD)
        for j in range(OWNERS):
            owner = c * OWNERS + j

            @pl.when(owner != me)
            def _():
                block_copy(owner).start()

            @pl.when(owner == me)
            def _():
                got[me] = tiles[owner]

    def last(i, carry):
        for way in (0, 1):
            hop(way, 3, places(i + HALF)[way], (lows[3], highs[3])[way]).wait_recv()
        take(3, i + HALF)
        for way in (0, 1):
            c = i + way * HALF
            hop(way, 4, c, far).wait_recv()
            finish(c)
        return carry

    lax.fori_loop(0, HALF, last, 0)

    lane16 = lax.broadcasted_iota(jnp.int32, (NBINS, HD), 1)
    bin_sum = jnp.sum(ebins[...], axis=1, keepdims=True)
    eng[me] = jnp.sum(jnp.where(lane16 == sub16, bin_sum, 0.0), axis=0, keepdims=True)

    for dy in FAR_FIRST_Y:
        for dx in FAR_FIRST_X:
            for dc in (1, 0):
                if dx or dy or dc:
                    pltpu.make_async_remote_copy(
                        src_ref=eng.at[me],
                        dst_ref=eng.at[me],
                        send_sem=gsend,
                        recv_sem=grecv,
                        device_id={"dp": device(dx, dy, 1 - core if dc else core)},
                        device_id_type=MESH,
                    ).start()

    def residual(c, carry):
        errb[c] = jnp.where(maskb[c] > 0.5, 0.0, acc[c]).astype(BF16)
        err_copy(c).start()
        return carry

    lax.fori_loop(0, NCH, residual, 0)

    for copy in loads[2:]:
        copy.wait()
    others = NDP - 1
    pltpu.make_async_copy(got.at[pl.ds(0, others)], got.at[pl.ds(0, others)], trecv).wait()
    parity = lax.rem(me, 2)
    block = got[...]
    want = (lax.broadcasted_iota(jnp.int32, (NDP, 8, HD), 1) + 8 * parity).astype(F32)
    hot = jnp.where(want == block[:, 6:7, :], 1.0, 0.0).astype(BF16).reshape(NDP * 8, HD)
    parts = split3(block.reshape(NDP * 8, HD))
    both = (dot_t(hot, parts[0]) + dot_t(hot, parts[1])) + dot_t(hot, parts[2])
    kept_sum = both[:REGION] + both[REGION:]

    lane1 = lax.broadcasted_iota(jnp.int32, (1, HD), 1)
    low1 = jnp.zeros((1, HD), jnp.int32)
    high1 = jnp.zeros((1, HD), jnp.int32)
    for b in range(NBINS):
        low1 = jnp.where(lane1 == b, edges[b], low1)
        high1 = jnp.where(lane1 == b, edges[b + 1], high1)
    width = jnp.where(lane1 < NBINS, high1 - low1, 1).astype(F32)
    own_row = me * REGION + lax.broadcasted_iota(jnp.int32, (REGION, HD), 0)
    in_bin = (own_row >= low1) & (own_row < high1)

    pltpu.make_async_copy(eng.at[pl.ds(0, others)], eng.at[pl.ds(0, others)], grecv).wait()
    energy = jnp.sum(eng[...], axis=0)
    normal = 1.0 / jnp.sqrt(energy / (float(NDP * HD) * width) + epsilon)
    scale = jnp.where(lane1 >= thr[...], normal, 1.0)
    row_scale = jnp.sum(jnp.where(in_bin, scale, 0.0), axis=1, keepdims=True)
    grad = kept_sum * row_scale
    moment_new = beta_first * state[0] + (1.0 - beta_first) * grad
    second_new = beta_second * state[1] + (1.0 - beta_second) * grad * grad
    first_hat = moment_new / (1.0 - beta_first**step_count)
    second_hat = second_new / (1.0 - beta_second**step_count)
    master = state[2]
    master_new = master - learn_rate * (
        first_hat / (jnp.sqrt(second_hat) + adam_epsilon) + decay_rate * master
    )
    wbuf[me] = master_new.astype(BF16)

    def weight_copy(slot, to, sem):
        return pltpu.make_async_remote_copy(
            src_ref=wbuf.at[slot],
            dst_ref=wbuf.at[slot],
            send_sem=wsend,
            recv_sem=sem,
            device_id={"dp": to},
            device_id_type=MESH,
        )

    for k in NEAR_FIRST[1:]:
        weight_copy(me, device(0, k, core), wa.at[k]).start()
    news[0] = moment_new
    news[1] = second_new
    news[2] = master_new
    outs = [
        pltpu.make_async_copy(news.at[0], mom_out, isem.at[5]),
        pltpu.make_async_copy(news.at[1], sec_out, isem.at[6]),
        pltpu.make_async_copy(news.at[2], mas_out, isem.at[7]),
    ]
    for k in NEAR_FIRST:
        slot = device(0, NY - k, core)
        if k:
            weight_copy(slot, partner, wa.at[k]).wait_recv()
        for d in (1, 3, 2):
            weight_copy(slot, device(d, 0, core), wb.at[d - 1, k]).start()
        weight_copy(slot, partner, wc.at[0, k]).start()
    for copy in outs:
        copy.start()

    def pass_on(d):
        for k in NEAR_FIRST:
            slot = device(NX - d, NY - k, core)
            weight_copy(slot, partner, wb.at[d - 1, k]).wait_recv()
            weight_copy(slot, partner, wc.at[d, k]).start()

    def share(d):
        for k in NEAR_FIRST:
            weight_copy(device(NX - d, NY - k, 1 - core), partner, wc.at[d, k]).wait_recv()
        where_x = lax.rem(x + NX - d, NX)
        total = None
        for part in range(NY // 2):
            c = where_x * (NY // 2) + part
            weight = wbuf[pl.ds(c * OWNERS, OWNERS)].reshape(CW, HD)
            one = dot(fbuf[:, c].reshape(NZ * TOK, CW), weight)
            total = one if total is None else total + one
        return total

    pass_on(1)
    pass_on(3)
    kacc[...] = share(0)
    pass_on(2)
    kacc[...] += share(1)
    kacc[...] += share(3)
    kout[...] = (kacc[...] + share(2)).astype(BF16)
    keys_copy = pltpu.make_async_copy(kout, keys_out, isem.at[0])
    keys_copy.start()

    for way in (0, 1):
        pltpu.make_async_copy(
            fbuf.at[pl.ds(0, 3)], fbuf.at[pl.ds(0, 3)], zsend.at[way, 0]
        ).wait()
        pltpu.make_async_copy(
            fbuf.at[0, pl.ds(0, HALF)], fbuf.at[0, pl.ds(0, HALF)], zsend.at[way, 1]
        ).wait()
    pltpu.make_async_copy(got.at[pl.ds(0, others)], got.at[pl.ds(0, others)], tsend).wait()
    pltpu.make_async_copy(eng.at[pl.ds(0, others)], eng.at[pl.ds(0, others)], gsend).wait()
    pltpu.make_async_copy(wbuf.at[pl.ds(0, others)], wbuf.at[pl.ds(0, others)], wsend).wait()
    for c in range(NCH):
        err_copy(c).wait()
    for copy in outs:
        copy.wait()
    keys_copy.wait()


def put_out(
    keys, err, mom, sec, mas, keys_to, err_to, mom_to, sec_to, mas_to,
    keys_at, err_at, state_at, arrive, leave,
):
    quarter = ROWS // 4
    routes = []
    for q in range(4):
        rows = pl.ds(q * quarter, quarter)
        routes.append((err.at[0, rows, :], err_at.at[rows, :], err_to.at[0, rows, :]))
    routes.append((keys, keys_at, keys_to))
    for k, (a, b) in enumerate(((mom, mom_to), (sec, sec_to), (mas, mas_to))):
        routes.append((a, state_at.at[k], b))
    first = [pltpu.make_async_copy(a, b, arrive.at[k]) for k, (a, b, _) in enumerate(routes)]
    second = [pltpu.make_async_copy(b, c, leave.at[k]) for k, (_, b, c) in enumerate(routes)]
    for copy in first:
        copy.start()
    for one, two in zip(first, second):
        one.wait()
        two.start()
    for copy in second:
        copy.wait()


def shards(features, key_grads, error_in, selected, bin_edges, threshold, moment, second, master):
    hbm = pl.BlockSpec(memory_space=pltpu.HBM)
    vmem = pl.BlockSpec(memory_space=pltpu.VMEM)
    smem = pl.BlockSpec(memory_space=pltpu.SMEM)
    dma = pltpu.SemaphoreType.DMA
    state_shape = jax.ShapeDtypeStruct((REGION, HD), F32)
    out_shape = (
        jax.ShapeDtypeStruct((NZ * TOK, HD), BF16),
        jax.ShapeDtypeStruct((1, ROWS, HD), BF16),
        state_shape,
        state_shape,
        state_shape,
    )
    results = pl.pallas_call(
        kernel,
        out_shape=out_shape,
        in_specs=[hbm, hbm, hbm, vmem, smem, vmem, hbm, hbm, hbm],
        out_specs=(hbm,) * 5,
        scratch_shapes=[
            pltpu.VMEM((NZ, NCH, TOK, CW), BF16),
            pltpu.VMEM((NZ * TOK, HD), BF16),
            pltpu.VMEM((ROWS, HD), BF16),
            pltpu.VMEM((NCH, CW, HD), F32),
            pltpu.VMEM((NCH, CW, HD), F32),
            pltpu.VMEM((NCH, NBINS, CW), BF16),
            pltpu.VMEM((32, 1, HD), F32),
            pltpu.VMEM((NCH, CW, HD), BF16),
            pltpu.VMEM((NBINS, HD), F32),
            pltpu.VMEM((NDP, 8, HD), F32),
            pltpu.VMEM((NDP, 8, HD), F32),
            pltpu.VMEM((NDP, 1, HD), F32),
            pltpu.VMEM((NDP, REGION, HD), BF16),
            pltpu.VMEM((NZ * TOK, HD), F32),
            pltpu.VMEM((NZ * TOK, HD), BF16),
            pltpu.VMEM((3, REGION, HD), F32),
            pltpu.VMEM((3, REGION, HD), F32),
            dma((NCH,)),
            dma((8,)),
            dma((NCH,)),
            pltpu.SemaphoreType.REGULAR((6,)),
            dma((2, 2)),
            dma((2, 4, NCH)),
            dma,
            dma,
            dma,
            dma,
            dma,
            dma((NY,)),
            dma((NX - 1, NY)),
            dma((NX, NY)),
        ],
        compiler_params=pltpu.CompilerParams(
            collective_id=0, has_side_effects=True, vmem_limit_bytes=58 * 1024 * 1024
        ),
        name="step",
    )(features, key_grads, error_in, selected, bin_edges, threshold.reshape(1, 1), moment, second, master)
    return pl.pallas_call(
        put_out,
        out_shape=out_shape,
        in_specs=[hbm] * 5,
        out_specs=(hbm,) * 5,
        scratch_shapes=[
            pltpu.VMEM((NZ * TOK, HD), BF16),
            pltpu.VMEM((ROWS, HD), BF16),
            pltpu.VMEM((3, REGION, HD), F32),
            dma((8,)),
            dma((8,)),
        ],
        compiler_params=pltpu.CompilerParams(vmem_limit_bytes=58 * 1024 * 1024),
        name="put_out",
    )(*results)


def solution(mesh):
    in_specs = (
        P(("dp", "tensor"), None),
        P("dp", "tensor"),
        P("dp", None, "tensor"),
        P("dp", "tensor", None),
        P(),
        P(),
        P("dp", "tensor"),
        P("dp", "tensor"),
        P("dp", "tensor"),
    )
    out_specs = (
        P("dp", "tensor"),
        P("dp", None, "tensor"),
        P("dp", "tensor"),
        P("dp", "tensor"),
        P("dp", "tensor"),
    )
    return jax.shard_map(shards, mesh=mesh, in_specs=in_specs, out_specs=out_specs, check_vma=False)
```
